32 devices in a mesh: col: 8 (over y, x, core), row: 4 (over z).
Axes of the slice: x: 2, y: 2, z: 4, core: 2. Of those that a mesh axis runs over, the one named last changes fastest.
Arguments:
- samples_x: bfloat16 [512, 98304], P('row', 'col'), may hold values from -6 to 6
- targets: bfloat16 [512, 98304], P('row', 'col'), may hold values from -6 to 6
- times: int32 [512], P('row'), may hold values from 0 to 63
- block_rows: int32 [576], P(('col', 'row')), may hold values from 0 to 767, as said below
- block_cols: int32 [576], P(('col', 'row')), may hold values from 0 to 767, as said below
Outputs:
- coeffs: float32 [576, 128, 128], P(('col', 'row'))
- residual: float32 [512, 98304], P('row', 'col')
The draws below stay inside these ranges and needn't reach their ends.
Inputs may be any that keep to these rules, and one draw needn't show every extreme that they name: `block_rows`: the blocks are listed by column group (the 96 column blocks c * 96 to (c + 1) * 96 - 1 form group c), and within a group in 8 runs of 9 blocks, run g holding row blocks of group g; no block appears twice. `block_cols`: each block's column block lies in the group of its place in the list, as described for block_rows.
All inputs are finite; a program needn't handle non-finite values.
Results may differ from the reference program's by a relative error of at most 0.009.
Values may be sent and summed in bfloat16 or wider, within the bound.
A program may use at most 192 MiB of HBM per device.

```python
import jax
import jax.numpy as jnp
from jax import lax

TAXA = 98304
BLOCK = 128
RUN = 9
SAMP_ROW = 128
ITERS = 2
T_STEPS = 64
CBLK = 96
BLOCKS = 576
SAMPLES = 512
N_COL = 8
N_ROW = 4


def pattern_pairs(key):
    keys = jax.random.split(jax.random.fold_in(key, 11), N_COL * N_COL)

    def one_run(run_key):
        return jax.random.permutation(run_key, CBLK * CBLK)[:RUN].astype(jnp.int32)
    picks = jax.vmap(one_run)(keys)
    grid = jnp.arange(N_COL * N_COL, dtype=jnp.int32)
    col_group = grid // N_COL
    src_group = grid % N_COL
    rows = src_group[:, None] * CBLK + picks // CBLK
    cols = col_group[:, None] * CBLK + picks % CBLK
    return (rows.reshape(-1).astype(jnp.int32), cols.reshape(-1).astype(jnp.int32))


def draw_block_rows(key, part):
    rows, cols = pattern_pairs(key)
    return rows


def draw_block_cols(key, part):
    rows, cols = pattern_pairs(key)
    return cols


def place_ends(entries, stream_key, low, high):
    dims = entries.shape
    place = [jax.random.randint(jax.random.fold_in(stream_key, axis), (), 0, dims[axis]) for axis in range(len(dims))]
    entries = entries.at[tuple(place)].set(low)
    longest = dims.index(max(dims))
    place[longest] = (place[longest] + 1) % dims[longest]
    return entries.at[tuple(place)].set(high)


def shard_levels(key, extent, cuts, least, top_value):
    level, own = 1.0, jax.random.fold_in(key, 6)
    for position, parts in cuts:
        heights = jnp.exp(jax.random.uniform(jax.random.fold_in(own, position), (parts,), jnp.float32, least / len(cuts), top_value / len(cuts)))
        level = level * jnp.repeat(heights, extent[position] // parts).reshape([-1 if axis == position else 1 for axis in range(len(extent))])
    return level


def noise(own_key, extent, scale, reach, cuts=(), kind=jnp.bfloat16):
    drawn = jax.random.normal(own_key, extent, jnp.float32) * scale
    if len(cuts) > 0:
        drawn = shard_levels(own_key, extent, cuts, -0.22, 0.18) * drawn
    return jnp.clip(drawn, min=-reach, max=reach).astype(kind)


def setup_inputs(seed: int = 0) -> dict:
    streams_of = jax.random.split(jax.random.key(seed), 6)
    samples_x = noise(streams_of[0], (SAMPLES, TAXA), 1.0, 6.0, ((0, 4), (1, 8)))
    targets = noise(streams_of[1], (SAMPLES, TAXA), 1.0, 6.0, ((0, 4), (1, 8)))
    times = place_ends(jax.random.randint(streams_of[2], (SAMPLES,), 0, T_STEPS), jax.random.fold_in(streams_of[2], 1), 0, T_STEPS - 1).astype(jnp.int32)
    block_rows = draw_block_rows(jax.random.fold_in(streams_of[5], 71), 0)
    block_cols = draw_block_cols(jax.random.fold_in(streams_of[5], 71), 0)
    return dict(samples_x=samples_x, targets=targets, times=times, block_rows=block_rows, block_cols=block_cols)


RIDGE_SHARE = 0.2


def reference(samples_x, targets, times, block_rows, block_cols):
    weight = (0.5 + times.astype(jnp.float32) / T_STEPS)[:, None]
    ridge = RIDGE_SHARE * SAMPLES
    block_count = TAXA // BLOCK
    x_blocks = samples_x.reshape(SAMPLES, block_count, BLOCK)
    x_groups = samples_x.reshape(N_ROW, SAMP_ROW, block_count, BLOCK)

    def adjoint(weighted):
        e_groups = weighted.reshape(N_ROW, SAMP_ROW, block_count, BLOCK)

        def one_group(total, pair):
            x_group, e_group = pair
            x_sel = jnp.take(x_group, block_rows, axis=1).astype(jnp.float32)
            e_sel = jnp.take(e_group, block_cols, axis=1).astype(jnp.float32)
            term = jnp.einsum("ska,skb->kab", x_sel, e_sel)
            rounded = lax.optimization_barrier(term.astype(jnp.bfloat16))
            return total + rounded.astype(jnp.float32), None

        start_total = jnp.zeros((BLOCKS, BLOCK, BLOCK), jnp.float32)
        total, unused = lax.scan(one_group, start_total, (x_groups, e_groups))
        return total

    def apply(direction):
        x_sel = jnp.take(x_blocks, block_rows, axis=1).astype(jnp.float32)
        contrib = jnp.einsum("ska,kab->skb", x_sel, direction.astype(jnp.float32))
        image = jnp.zeros((SAMPLES, block_count, BLOCK), jnp.float32).at[:, block_cols].add(contrib)
        return image.reshape(SAMPLES, TAXA)

    start = (targets.astype(jnp.float32) * weight).astype(jnp.bfloat16)
    gradient = adjoint(start)
    gamma = jnp.sum(gradient * gradient)
    direction = gradient.astype(jnp.bfloat16)
    coeffs = jnp.zeros((BLOCKS, BLOCK, BLOCK), jnp.float32)
    residual = targets.astype(jnp.float32)
    for step in range(ITERS):
        image = apply(direction)
        flat = direction.astype(jnp.float32)
        alpha = gamma / (jnp.sum(weight * image * image) + ridge * jnp.sum(flat * flat))
        coeffs = coeffs + alpha * flat
        residual = residual - alpha * image
        if step + 1 < ITERS:
            gradient = adjoint((residual * weight).astype(jnp.bfloat16)) - ridge * coeffs
            gamma_next = jnp.sum(gradient * gradient)
            direction = (gradient + (gamma_next / gamma) * flat).astype(jnp.bfloat16)
            gamma = gamma_next
    return coeffs, residual
```

```python
import functools
import math

import jax
import jax.numpy as jnp
from jax import lax
from jax.experimental import pallas as pl
from jax.experimental.pallas import tpu as pltpu
from jax.sharding import PartitionSpec as P

BLOCK = 128
T_STEPS = 64
RIDGE_SHARE = 0.2
LANES = 128
VMEM = pltpu.VMEM
F32 = jnp.float32
BF16 = jnp.bfloat16
WHOLE = pl.BlockSpec(memory_space=pltpu.VMEM)
SCALARS = pl.BlockSpec(memory_space=pltpu.SMEM)


def enter(axes):
    barrier = pltpu.get_barrier_semaphore()
    count = 0
    for axis in axes:
        n = lax.axis_size(axis)
        me = lax.axis_index(axis)
        for k in range(1, n):
            pl.semaphore_signal(
                barrier, inc=1, device_id={axis: lax.rem(me + k, n)},
                device_id_type=pl.DeviceIdType.MESH,
            )
        count += n - 1
    pl.semaphore_wait(barrier, count)


def push(src, dst, send, recv, axis, k):
    n = lax.axis_size(axis)
    return pltpu.make_async_remote_copy(
        src_ref=src, dst_ref=dst, send_sem=send, recv_sem=recv,
        device_id={axis: lax.rem(lax.axis_index(axis) + k, n)},
        device_id_type=pl.DeviceIdType.MESH,
    )


def gather_small_kernel(x_ref, out_ref, send_c, recv_c, send_r, recv_r):
    cols, rows = lax.axis_size("col"), lax.axis_size("row")
    my_col, my_row = lax.axis_index("col"), lax.axis_index("row")
    enter(("col", "row"))
    out_ref[my_row, my_col] = x_ref[...]
    first = [
        push(x_ref, out_ref.at[my_row, my_col], send_c.at[k - 1], recv_c.at[k - 1], "col", k)
        for k in range(1, cols)
    ]
    for copy in first:
        copy.start()
    for copy in first:
        copy.wait()
    second = [
        push(out_ref.at[my_row], out_ref.at[my_row], send_r.at[k - 1], recv_r.at[k - 1], "row", k)
        for k in range(1, rows)
    ]
    for copy in second:
        copy.start()
    for copy in second:
        copy.wait()


def gather_small(x, call_id):
    cols, rows = lax.axis_size("col"), lax.axis_size("row")
    return pl.pallas_call(
        gather_small_kernel,
        out_shape=jax.ShapeDtypeStruct((rows, cols) + x.shape, x.dtype),
        in_specs=[WHOLE],
        out_specs=WHOLE,
        scratch_shapes=[
            pltpu.SemaphoreType.DMA((cols - 1,)), pltpu.SemaphoreType.DMA((cols - 1,)),
            pltpu.SemaphoreType.DMA((rows - 1,)), pltpu.SemaphoreType.DMA((rows - 1,)),
        ],
        compiler_params=pltpu.CompilerParams(collective_id=call_id, has_side_effects=True),
    )(x)


def select_kernel(run, index_ref, x_ref, out_ref):
    def one(b, carry):
        column = pl.multiple_of(index_ref[b] * BLOCK, BLOCK)
        out_ref[b] = x_ref[:, pl.ds(column, BLOCK)]
        return carry

    lax.fori_loop(0, out_ref.shape[0], one, 0, unroll=2)


def select_blocks(index, x):
    count = index.shape[0]
    return pl.pallas_call(
        functools.partial(select_kernel, count),
        out_shape=jax.ShapeDtypeStruct((count, x.shape[0], BLOCK), x.dtype),
        in_specs=[SCALARS, WHOLE],
        out_specs=WHOLE,
    )(index, x)


def exchange_kernel(run, x_ref, out_ref, send, recv):
    n, me = lax.axis_size("col"), lax.axis_index("col")
    enter(("col",))
    copies = []
    for k in range(1, n):
        peer = lax.rem(me + k, n)
        copies.append(
            push(x_ref.at[pl.ds(peer * run, run)], out_ref.at[pl.ds(me * run, run)],
                 send.at[k - 1], recv.at[k - 1], "col", k)
        )
    for copy in copies:
        copy.start()

    def own(i, carry):
        out_ref[me * run + i] = x_ref[me * run + i]
        return carry

    lax.fori_loop(0, run, own, 0)
    for copy in copies:
        copy.wait()


def exchange_blocks(x, call_id):
    n = lax.axis_size("col")
    return pl.pallas_call(
        functools.partial(exchange_kernel, x.shape[0] // n),
        out_shape=jax.ShapeDtypeStruct(x.shape, x.dtype),
        in_specs=[WHOLE],
        out_specs=WHOLE,
        scratch_shapes=[pltpu.SemaphoreType.DMA((n - 1,)), pltpu.SemaphoreType.DMA((n - 1,))],
        compiler_params=pltpu.CompilerParams(collective_id=call_id, has_side_effects=True),
    )(x)


def block_dot(x, e):
    return lax.dot_general(x, e, (((0,), (0,)), ((), ())), preferred_element_type=F32)


def unroll_of(count):
    return math.gcd(count, 4)


def first_terms_kernel(cols_ref, x_ref, t_ref, w_ref, out_ref):
    count = x_ref.shape[0]
    step = unroll_of(count)

    def some(i, carry):
        for j in range(step):
            b = i * step + j
            place = pl.ds(pl.multiple_of(cols_ref[b] * BLOCK, BLOCK), BLOCK)
            e = (t_ref[:, place].astype(F32) * w_ref[...]).astype(BF16)
            out_ref[b] = block_dot(x_ref[b], e).astype(BF16)
        return carry

    lax.fori_loop(0, count // step, some, 0)


def first_terms(cols, x, targets, weight):
    return pl.pallas_call(
        first_terms_kernel,
        out_shape=jax.ShapeDtypeStruct((x.shape[0], BLOCK, BLOCK), BF16),
        in_specs=[SCALARS, WHOLE, WHOLE, WHOLE],
        out_specs=WHOLE,
    )(cols, x, targets, weight)


def next_terms_kernel(cols_ref, scale_ref, x_ref, t_ref, image_ref, w_ref, out_ref):
    count = x_ref.shape[0]
    step = unroll_of(count)
    alpha = scale_ref[0]

    def some(i, carry):
        for j in range(step):
            b = i * step + j
            place = pl.ds(pl.multiple_of(cols_ref[b] * BLOCK, BLOCK), BLOCK)
            left = t_ref[:, place].astype(F32) - alpha * image_ref[:, place]
            out_ref[b] = block_dot(x_ref[b], (left * w_ref[...]).astype(BF16)).astype(BF16)
        return carry

    lax.fori_loop(0, count // step, some, 0)


def next_terms(cols, scale, x, targets, image, weight):
    return pl.pallas_call(
        next_terms_kernel,
        out_shape=jax.ShapeDtypeStruct((x.shape[0], BLOCK, BLOCK), BF16),
        in_specs=[SCALARS, SCALARS, WHOLE, WHOLE, WHOLE, WHOLE],
        out_specs=WHOLE,
    )(cols, scale, x, targets, image, weight)


def reduce_gather_kernel(pieces, first, *refs):
    if first:
        terms_ref, out_ref, own_ref, sums_ref, held, rs_send, rs_recv, ag_send, ag_recv = refs
        before_ref = None
        shift = None
    else:
        (scale_ref, terms_ref, before_ref, out_ref, own_ref, sums_ref, held,
         rs_send, rs_recv, ag_send, ag_recv) = refs
        shift = scale_ref[1]
    n, me = lax.axis_size("row"), lax.axis_index("row")
    share = own_ref.shape[0]
    size = share // pieces
    enter(("row",))
    scatter, spread = [], []
    for p in range(pieces):
        part = []
        for k in range(1, n):
            peer = lax.rem(me + k, n)
            part.append(
                push(terms_ref.at[pl.ds(peer * share + p * size, size)],
                     held.at[k - 1, pl.ds(p * size, size)],
                     rs_send.at[p, k - 1], rs_recv.at[p, k - 1], "row", k)
            )
        for copy in part:
            copy.start()
        scatter.append(part)
    sums_ref[...] = jnp.zeros_like(sums_ref)
    for p in range(pieces):
        for copy in scatter[p]:
            copy.wait_recv()

        def one(i, carry):
            total = terms_ref[me * share + i].astype(F32)
            for k in range(1, n):
                total = total + held[k - 1, i].astype(F32)
            if before_ref is not None:
                flat = before_ref[i].astype(F32)
                total = total - shift * flat
            rounded = total.astype(BF16)
            own_ref[i] = rounded
            out_ref[me * share + i] = rounded
            wide = rounded.astype(F32)
            sums_ref[0:1, :] += jnp.sum(total * total, axis=0, keepdims=True)
            sums_ref[1:2, :] += jnp.sum(wide * wide, axis=0, keepdims=True)
            if before_ref is not None:
                sums_ref[2:3, :] += jnp.sum(wide * flat, axis=0, keepdims=True)
            return carry

        lax.fori_loop(p * size, (p + 1) * size, one, 0)
        part = [
            push(own_ref.at[pl.ds(p * size, size)],
                 out_ref.at[pl.ds(me * share + p * size, size)],
                 ag_send.at[p, k - 1], ag_recv.at[p, k - 1], "row", k)
            for k in range(1, n)
        ]
        for copy in part:
            copy.start()
        spread.append(part)
    for part in scatter:
        for copy in part:
            copy.wait_send()
    for part in spread:
        for copy in part:
            copy.wait()


def reduce_gather(terms, scale, before, call_id):
    n = lax.axis_size("row")
    share = terms.shape[0] // n
    pieces = math.gcd(share, 3)
    first = before is None
    sems = pltpu.SemaphoreType.DMA((pieces, n - 1))
    return pl.pallas_call(
        functools.partial(reduce_gather_kernel, pieces, first),
        out_shape=(
            jax.ShapeDtypeStruct(terms.shape, BF16),
            jax.ShapeDtypeStruct((share, BLOCK, BLOCK), BF16),
            jax.ShapeDtypeStruct((8, LANES), F32),
        ),
        in_specs=[WHOLE] if first else [SCALARS, WHOLE, WHOLE],
        out_specs=(WHOLE, WHOLE, WHOLE),
        scratch_shapes=[VMEM((n - 1, share, BLOCK, BLOCK), BF16), sems, sems, sems, sems],
        compiler_params=pltpu.CompilerParams(collective_id=call_id, has_side_effects=True),
    )(*((terms,) if first else (scale, terms, before)))


def apply_kernel(first, cols_ref, x_ref, d_ref, w_ref, *refs):
    if first:
        image_ref, sums_ref = refs
        before_ref = None
    else:
        before_ref, image_ref, sums_ref = refs
    count = x_ref.shape[0]
    step = unroll_of(count)
    columns = image_ref.shape[1] // BLOCK
    samples = image_ref.shape[0]

    def clear(i, carry):
        place = pl.ds(pl.multiple_of(i * BLOCK, BLOCK), BLOCK)
        image_ref[:, place] = jnp.zeros((samples, BLOCK), F32)
        return carry

    lax.fori_loop(0, columns, clear, 0, unroll=2)

    def some(i, carry):
        made = [
            jnp.dot(x_ref[i * step + j], d_ref[i * step + j], preferred_element_type=F32)
            for j in range(step)
        ]
        for j in range(step):
            place = pl.ds(pl.multiple_of(cols_ref[i * step + j] * BLOCK, BLOCK), BLOCK)
            image_ref[:, place] += made[j]
        return carry

    lax.fori_loop(0, count // step, some, 0)
    sums_ref[...] = jnp.zeros_like(sums_ref)

    def measure(i, carry):
        place = pl.ds(pl.multiple_of(i * BLOCK, BLOCK), BLOCK)
        image = image_ref[:, place]
        weighted = w_ref[...] * image
        sums_ref[0:1, :] += jnp.sum(weighted * image, axis=0, keepdims=True)
        if before_ref is not None:
            sums_ref[1:2, :] += jnp.sum(weighted * before_ref[:, place], axis=0, keepdims=True)
        return carry

    lax.fori_loop(0, columns, measure, 0, unroll=2)


def apply_blocks(cols, x, direction, weight, before, taxa):
    first = before is None
    samples = x.shape[1]
    return pl.pallas_call(
        functools.partial(apply_kernel, first),
        out_shape=(
            jax.ShapeDtypeStruct((samples, taxa), F32),
            jax.ShapeDtypeStruct((8, LANES), F32),
        ),
        in_specs=[SCALARS] + [WHOLE] * (3 if first else 4),
        out_specs=(WHOLE, WHOLE),
    )(cols, x, direction, weight, *(() if first else (before,)))


def on_device(samples_x, targets, times, block_rows, block_cols):
    col_count = lax.axis_size("col")
    row_count = lax.axis_size("row")
    taxa_col = samples_x.shape[1]
    sample_count = samples_x.shape[0]
    column_count = taxa_col // BLOCK
    my_col = lax.axis_index("col")
    my_row = lax.axis_index("row")
    shard = block_rows.shape[0]
    group_count = shard * row_count
    run = group_count // col_count
    ridge = RIDGE_SHARE * sample_count * row_count
    weight = jnp.broadcast_to(
        (0.5 + times.astype(F32) / T_STEPS)[:, None], (sample_count, BLOCK)
    )
    places = jnp.pad(
        jnp.stack([block_rows, block_cols]), ((0, 6), (0, LANES - shard))
    )
    everywhere = gather_small(places, 1)
    rows_all = everywhere[:, :, 0, :shard].transpose(1, 0, 2).reshape(col_count, group_count)
    wanted = lax.dynamic_slice_in_dim(rows_all, my_col * run, run, 1) - my_col * column_count
    cols_mine = lax.dynamic_index_in_dim(everywhere[:, :, 1, :shard], my_col, 1, keepdims=False)
    cols = cols_mine.reshape(group_count) - my_col * column_count

    x = exchange_blocks(select_blocks(wanted.reshape(-1), samples_x), 2)
    terms = first_terms(cols, x, targets, weight)
    direction, own0, sums0 = reduce_gather(terms, None, None, 3)
    image0, norms0 = apply_blocks(cols, x, direction, weight, None, taxa_col)
    totals = jnp.sum(
        gather_small(jnp.concatenate([sums0[:2], norms0[:1], jnp.zeros((5, LANES), F32)]), 4),
        axis=(0, 1, 3),
    )
    gamma, flat_norm, image_norm = totals[0], totals[1], totals[2]
    alpha0 = gamma / (image_norm + ridge * flat_norm)
    scale = jnp.stack([alpha0, ridge * alpha0])
    terms = next_terms(cols, scale, x, targets, image0, weight)
    spread, own1, sums1 = reduce_gather(terms, scale, own0, 5)
    image1, norms1 = apply_blocks(cols, x, spread, weight, image0, taxa_col)
    totals = jnp.sum(
        gather_small(jnp.concatenate([sums1[:3], norms1[:2], jnp.zeros((3, LANES), F32)]), 6),
        axis=(0, 1, 3),
    )
    beta = totals[0] / gamma
    flat_next = totals[1] + 2.0 * beta * totals[2] + beta * beta * flat_norm
    image_next = totals[3] + 2.0 * beta * totals[4] + beta * beta * image_norm
    alpha1 = totals[0] / (image_next + ridge * flat_next)
    mixed = alpha0 + alpha1 * beta
    coeffs = mixed * own0.astype(F32) + alpha1 * own1.astype(F32)
    residual = targets.astype(F32) - mixed * image0 - alpha1 * image1
    return (coeffs, residual)


def solution(mesh):
    placed = (P("row", "col"), P("row", "col"), P("row"), P(("col", "row")), P(("col", "row")))
    return jax.shard_map(
        on_device,
        mesh=mesh,
        in_specs=placed,
        out_specs=(P(("col", "row"), None, None), P("row", "col")),
        check_vma=False,
    )
```

```python
import functools
import math

import jax
import jax.numpy as jnp
from jax import lax
from jax.experimental import pallas as pl
from jax.experimental.pallas import tpu as pltpu
from jax.sharding import PartitionSpec as P

BLOCK = 128
T_STEPS = 64
RIDGE_SHARE = 0.2
LANES = 128
VMEM = pltpu.VMEM
F32 = jnp.float32
BF16 = jnp.bfloat16
WHOLE = pl.BlockSpec(memory_space=pltpu.VMEM)
SCALARS = pl.BlockSpec(memory_space=pltpu.SMEM)


def enter(axes):
    barrier = pltpu.get_barrier_semaphore()
    count = 0
    for axis in axes:
        n = lax.axis_size(axis)
        me = lax.axis_index(axis)
        for k in range(1, n):
            pl.semaphore_signal(
                barrier, inc=1, device_id={axis: lax.rem(me + k, n)},
                device_id_type=pl.DeviceIdType.MESH,
            )
        count += n - 1
    pl.semaphore_wait(barrier, count)


def push(src, dst, send, recv, axis, k):
    n = lax.axis_size(axis)
    return pltpu.make_async_remote_copy(
        src_ref=src, dst_ref=dst, send_sem=send, recv_sem=recv,
        device_id={axis: lax.rem(lax.axis_index(axis) + k, n)},
        device_id_type=pl.DeviceIdType.MESH,
    )


def gather_small_kernel(x_ref, out_ref, send_c, recv_c, send_r, recv_r):
    cols, rows = lax.axis_size("col"), lax.axis_size("row")
    my_col, my_row = lax.axis_index("col"), lax.axis_index("row")
    enter(("col", "row"))
    out_ref[my_row, my_col] = x_ref[...]
    first = [
        push(x_ref, out_ref.at[my_row, my_col], send_c.at[k - 1], recv_c.at[k - 1], "col", k)
        for k in range(1, cols)
    ]
    for copy in first:
        copy.start()
    for copy in first:
        copy.wait()
    second = [
        push(out_ref.at[my_row], out_ref.at[my_row], send_r.at[k - 1], recv_r.at[k - 1], "row", k)
        for k in range(1, rows)
    ]
    for copy in second:
        copy.start()
    for copy in second:
        copy.wait()


def gather_small(x, call_id):
    cols, rows = lax.axis_size("col"), lax.axis_size("row")
    return pl.pallas_call(
        gather_small_kernel,
        out_shape=jax.ShapeDtypeStruct((rows, cols) + x.shape, x.dtype),
        in_specs=[WHOLE],
        out_specs=WHOLE,
        scratch_shapes=[
            pltpu.SemaphoreType.DMA((cols - 1,)), pltpu.SemaphoreType.DMA((cols - 1,)),
            pltpu.SemaphoreType.DMA((rows - 1,)), pltpu.SemaphoreType.DMA((rows - 1,)),
        ],
        compiler_params=pltpu.CompilerParams(collective_id=call_id, has_side_effects=True),
    )(x)


def select_kernel(run, index_ref, x_ref, out_ref):
    def one(b, carry):
        column = pl.multiple_of(index_ref[b] * BLOCK, BLOCK)
        out_ref[b] = x_ref[:, pl.ds(column, BLOCK)]
        return carry

    lax.fori_loop(0, out_ref.shape[0], one, 0, unroll=2)


def select_blocks(index, x):
    count = index.shape[0]
    return pl.pallas_call(
        functools.partial(select_kernel, count),
        out_shape=jax.ShapeDtypeStruct((count, x.shape[0], BLOCK), x.dtype),
        in_specs=[SCALARS, WHOLE],
        out_specs=WHOLE,
    )(index, x)


def exchange_kernel(run, x_ref, out_ref, send, recv):
    n, me = lax.axis_size("col"), lax.axis_index("col")
    enter(("col",))
    copies = []
    for k in range(1, n):
        peer = lax.rem(me + k, n)
        copies.append(
            push(x_ref.at[pl.ds(peer * run, run)], out_ref.at[pl.ds(me * run, run)],
                 send.at[k - 1], recv.at[k - 1], "col", k)
        )
    for copy in copies:
        copy.start()

    def own(i, carry):
        out_ref[me * run + i] = x_ref[me * run + i]
        return carry

    lax.fori_loop(0, run, own, 0)
    for copy in copies:
        copy.wait()


def exchange_blocks(x, call_id):
    n = lax.axis_size("col")
    return pl.pallas_call(
        functools.partial(exchange_kernel, x.shape[0] // n),
        out_shape=jax.ShapeDtypeStruct(x.shape, x.dtype),
        in_specs=[WHOLE],
        out_specs=WHOLE,
        scratch_shapes=[pltpu.SemaphoreType.DMA((n - 1,)), pltpu.SemaphoreType.DMA((n - 1,))],
        compiler_params=pltpu.CompilerParams(collective_id=call_id, has_side_effects=True),
    )(x)


def block_dot(x, e):
    return lax.dot_general(x, e, (((0,), (0,)), ((), ())), preferred_element_type=F32)


def unroll_of(count):
    return math.gcd(count, 4)


def first_terms_kernel(cols_ref, x_ref, t_ref, w_ref, out_ref):
    count = x_ref.shape[0]
    step = unroll_of(count)

    def some(i, carry):
        for j in range(step):
            b = i * step + j
            place = pl.ds(pl.multiple_of(cols_ref[b] * BLOCK, BLOCK), BLOCK)
            e = (t_ref[:, place].astype(F32) * w_ref[...]).astype(BF16)
            out_ref[b] = block_dot(x_ref[b], e).astype(BF16)
        return carry

    lax.fori_loop(0, count // step, some, 0)


def first_terms(cols, x, targets, weight):
    return pl.pallas_call(
        first_terms_kernel,
        out_shape=jax.ShapeDtypeStruct((x.shape[0], BLOCK, BLOCK), BF16),
        in_specs=[SCALARS, WHOLE, WHOLE, WHOLE],
        out_specs=WHOLE,
    )(cols, x, targets, weight)


def next_terms_kernel(cols_ref, scale_ref, x_ref, t_ref, image_ref, w_ref, out_ref):
    count = x_ref.shape[0]
    step = unroll_of(count)
    alpha = scale_ref[0]

    def some(i, carry):
        for j in range(step):
            b = i * step + j
            place = pl.ds(pl.multiple_of(cols_ref[b] * BLOCK, BLOCK), BLOCK)
            left = t_ref[:, place].astype(F32) - alpha * image_ref[:, place]
            out_ref[b] = block_dot(x_ref[b], (left * w_ref[...]).astype(BF16)).astype(BF16)
        return carry

    lax.fori_loop(0, count // step, some, 0)


def next_terms(cols, scale, x, targets, image, weight):
    return pl.pallas_call(
        next_terms_kernel,
        out_shape=jax.ShapeDtypeStruct((x.shape[0], BLOCK, BLOCK), BF16),
        in_specs=[SCALARS, SCALARS, WHOLE, WHOLE, WHOLE, WHOLE],
        out_specs=WHOLE,
    )(cols, scale, x, targets, image, weight)


def sweep_kernel(first, *refs):
    if first:
        (terms_ref, out_ref, own_ref, sums_ref, from_left, from_right, to_right, to_left,
         send_r, recv_r, send_l, recv_l) = refs
        before_ref = None
    else:
        (scale_ref, terms_ref, before_ref, out_ref, own_ref, sums_ref, from_left, from_right,
         to_right, to_left, send_r, recv_r, send_l, recv_l) = refs
        shift = scale_ref[1]
    n, me = lax.axis_size("row"), lax.axis_index("row")
    pieces = send_r.shape[0]
    size = terms_ref.shape[0] // pieces
    share = own_ref.shape[0]
    has_left, has_right = me > 0, me < n - 1
    barrier = pltpu.get_barrier_semaphore()

    def greet(k):
        pl.semaphore_signal(
            barrier, inc=1, device_id={"row": lax.rem(me + k, n)},
            device_id_type=pl.DeviceIdType.MESH,
        )

    pl.when(has_left)(lambda: greet(n - 1))
    pl.when(has_right)(lambda: greet(1))
    pl.semaphore_wait(barrier, has_left.astype(jnp.int32) + has_right.astype(jnp.int32))

    def rightward(src, p):
        place = pl.ds(p * size, size)
        return push(src.at[place], from_left.at[place], send_r.at[p], recv_r.at[p], "row", 1)

    def leftward(src, p):
        place = pl.ds(p * size, size)
        return push(src.at[place], from_right.at[place], send_l.at[p], recv_l.at[p], "row", n - 1)

    def begin(source, heading):
        def one(p, carry):
            heading(source, p).start()
            return carry

        lax.fori_loop(0, pieces, one, 0)

    def clear(buffer):
        def one(i, carry):
            buffer[i] = jnp.zeros((BLOCK, BLOCK), BF16)
            return carry

        lax.fori_loop(0, buffer.shape[0], one, 0)

    @pl.when(me == 0)
    def _():
        begin(terms_ref, rightward)
        clear(from_left)

    @pl.when(me == n - 1)
    def _():
        begin(terms_ref, leftward)
        clear(from_right)

    def add(arrived, staged, p):
        def one(i, carry):
            b = p * size + i
            staged[b] = (arrived[b].astype(F32) + terms_ref[b].astype(F32)).astype(BF16)
            return carry

        lax.fori_loop(0, size, one, 0)

    def total_of(b):
        total = terms_ref[b].astype(F32) + from_left[b].astype(F32) + from_right[b].astype(F32)
        if before_ref is not None:
            total = total - shift * before_ref[b].astype(F32)
        return total

    def piece(p, carry):
        @pl.when(has_left)
        def _():
            rightward(to_right, p).wait_recv()

            @pl.when(has_right)
            def _():
                add(from_left, to_right, p)
                rightward(to_right, p).start()

        @pl.when(has_right)
        def _():
            leftward(to_left, p).wait_recv()

            @pl.when(has_left)
            def _():
                add(from_right, to_left, p)
                leftward(to_left, p).start()

        def one(i, inner):
            b = p * size + i
            out_ref[b] = total_of(b).astype(BF16)
            return inner

        lax.fori_loop(0, size, one, 0)
        return carry

    lax.fori_loop(0, pieces, piece, 0)
    sums_ref[...] = jnp.zeros_like(sums_ref)

    def own(i, carry):
        b = me * share + i
        total = total_of(b)
        rounded = total.astype(BF16)
        own_ref[i] = rounded
        wide = rounded.astype(F32)
        sums_ref[0:1, :] += jnp.sum(total * total, axis=0, keepdims=True)
        sums_ref[1:2, :] += jnp.sum(wide * wide, axis=0, keepdims=True)
        if before_ref is not None:
            flat = before_ref[b].astype(F32)
            sums_ref[2:3, :] += jnp.sum(wide * flat, axis=0, keepdims=True)
        return carry

    lax.fori_loop(0, share, own, 0)

    def finish(p, carry):
        pl.when(has_right)(lambda: rightward(to_right, p).wait_send())
        pl.when(has_left)(lambda: leftward(to_left, p).wait_send())
        return carry

    lax.fori_loop(0, pieces, finish, 0)


def sweep(terms, scale, before, call_id):
    n = lax.axis_size("row")
    share = terms.shape[0] // n
    pieces = math.gcd(terms.shape[0], 12)
    first = before is None
    sems = pltpu.SemaphoreType.DMA((pieces,))
    whole = VMEM(terms.shape, BF16)
    return pl.pallas_call(
        functools.partial(sweep_kernel, first),
        out_shape=(
            jax.ShapeDtypeStruct(terms.shape, BF16),
            jax.ShapeDtypeStruct((share, BLOCK, BLOCK), BF16),
            jax.ShapeDtypeStruct((8, LANES), F32),
        ),
        in_specs=[WHOLE] if first else [SCALARS, WHOLE, WHOLE],
        out_specs=(WHOLE, WHOLE, WHOLE),
        scratch_shapes=[whole, whole, whole, whole, sems, sems, sems, sems],
        compiler_params=pltpu.CompilerParams(collective_id=call_id, has_side_effects=True),
    )(*((terms,) if first else (scale, terms, before)))


def apply_kernel(first, cols_ref, x_ref, d_ref, w_ref, *refs):
    if first:
        image_ref, sums_ref = refs
        before_ref = None
    else:
        before_ref, image_ref, sums_ref = refs
    count = x_ref.shape[0]
    step = unroll_of(count)
    columns = image_ref.shape[1] // BLOCK
    samples = image_ref.shape[0]

    def clear(i, carry):
        place = pl.ds(pl.multiple_of(i * BLOCK, BLOCK), BLOCK)
        image_ref[:, place] = jnp.zeros((samples, BLOCK), F32)
        return carry

    lax.fori_loop(0, columns, clear, 0, unroll=2)

    def some(i, carry):
        made = [
            jnp.dot(x_ref[i * step + j], d_ref[i * step + j], preferred_element_type=F32)
            for j in range(step)
        ]
        for j in range(step):
            place = pl.ds(pl.multiple_of(cols_ref[i * step + j] * BLOCK, BLOCK), BLOCK)
            image_ref[:, place] += made[j]
        return carry

    lax.fori_loop(0, count // step, some, 0)
    sums_ref[...] = jnp.zeros_like(sums_ref)

    def measure(i, carry):
        place = pl.ds(pl.multiple_of(i * BLOCK, BLOCK), BLOCK)
        image = image_ref[:, place]
        weighted = w_ref[...] * image
        sums_ref[0:1, :] += jnp.sum(weighted * image, axis=0, keepdims=True)
        if before_ref is not None:
            sums_ref[1:2, :] += jnp.sum(weighted * before_ref[:, place], axis=0, keepdims=True)
        return carry

    lax.fori_loop(0, columns, measure, 0, unroll=2)


def apply_blocks(cols, x, direction, weight, before, taxa):
    first = before is None
    samples = x.shape[1]
    return pl.pallas_call(
        functools.partial(apply_kernel, first),
        out_shape=(
            jax.ShapeDtypeStruct((samples, taxa), F32),
            jax.ShapeDtypeStruct((8, LANES), F32),
        ),
        in_specs=[SCALARS] + [WHOLE] * (3 if first else 4),
        out_specs=(WHOLE, WHOLE),
    )(cols, x, direction, weight, *(() if first else (before,)))


def on_device(samples_x, targets, times, block_rows, block_cols):
    col_count = lax.axis_size("col")
    row_count = lax.axis_size("row")
    taxa_col = samples_x.shape[1]
    sample_count = samples_x.shape[0]
    column_count = taxa_col // BLOCK
    my_col = lax.axis_index("col")
    shard = block_rows.shape[0]
    group_count = shard * row_count
    run = group_count // col_count
    ridge = RIDGE_SHARE * sample_count * row_count
    weight = jnp.broadcast_to(
        (0.5 + times.astype(F32) / T_STEPS)[:, None], (sample_count, BLOCK)
    )
    places = jnp.pad(
        jnp.stack([block_rows, block_cols]), ((0, 6), (0, LANES - shard))
    )
    everywhere = gather_small(places, 1)
    rows_all = everywhere[:, :, 0, :shard].transpose(1, 0, 2).reshape(col_count, group_count)
    wanted = lax.dynamic_slice_in_dim(rows_all, my_col * run, run, 1) - my_col * column_count
    cols_mine = lax.dynamic_index_in_dim(everywhere[:, :, 1, :shard], my_col, 1, keepdims=False)
    cols = cols_mine.reshape(group_count) - my_col * column_count

    x = exchange_blocks(select_blocks(wanted.reshape(-1), samples_x), 2)
    terms = first_terms(cols, x, targets, weight)
    direction, own0, sums0 = sweep(terms, None, None, 3)
    image0, norms0 = apply_blocks(cols, x, direction, weight, None, taxa_col)
    totals = jnp.sum(
        gather_small(jnp.concatenate([sums0[:2], norms0[:1], jnp.zeros((5, LANES), F32)]), 4),
        axis=(0, 1, 3),
    )
    gamma, flat_norm, image_norm = totals[0], totals[1], totals[2]
    alpha0 = gamma / (image_norm + ridge * flat_norm)
    scale = jnp.stack([alpha0, ridge * alpha0])
    terms = next_terms(cols, scale, x, targets, image0, weight)
    spread, own1, sums1 = sweep(terms, scale, direction, 5)
    image1, norms1 = apply_blocks(cols, x, spread, weight, image0, taxa_col)
    totals = jnp.sum(
        gather_small(jnp.concatenate([sums1[:3], norms1[:2], jnp.zeros((3, LANES), F32)]), 6),
        axis=(0, 1, 3),
    )
    beta = totals[0] / gamma
    flat_next = totals[1] + 2.0 * beta * totals[2] + beta * beta * flat_norm
    image_next = totals[3] + 2.0 * beta * totals[4] + beta * beta * image_norm
    alpha1 = totals[0] / (image_next + ridge * flat_next)
    mixed = alpha0 + alpha1 * beta
    coeffs = mixed * own0.astype(F32) + alpha1 * own1.astype(F32)
    residual = targets.astype(F32) - mixed * image0 - alpha1 * image1
    return (coeffs, residual)


def solution(mesh):
    placed = (P("row", "col"), P("row", "col"), P("row"), P(("col", "row")), P(("col", "row")))
    return jax.shard_map(
        on_device,
        mesh=mesh,
        in_specs=placed,
        out_specs=(P(("col", "row"), None, None), P("row", "col")),
        check_vma=False,
    )
```

```python
import functools
import math

import jax
import jax.numpy as jnp
from jax import lax
from jax.experimental import pallas as pl
from jax.experimental.pallas import tpu as pltpu
from jax.sharding import PartitionSpec as P

BLOCK = 128
T_STEPS = 64
RIDGE_SHARE = 0.2
LANES = 128
LAG = 2
VMEM = pltpu.VMEM
F32 = jnp.float32
BF16 = jnp.bfloat16
WHOLE = pl.BlockSpec(memory_space=pltpu.VMEM)
SCALARS = pl.BlockSpec(memory_space=pltpu.SMEM)


def enter(axes):
    barrier = pltpu.get_barrier_semaphore()
    count = 0
    for axis in axes:
        n = lax.axis_size(axis)
        me = lax.axis_index(axis)
        for k in range(1, n):
            pl.semaphore_signal(
                barrier, inc=1, device_id={axis: lax.rem(me + k, n)},
                device_id_type=pl.DeviceIdType.MESH,
            )
        count += n - 1
    pl.semaphore_wait(barrier, count)


def push(src, dst, send, recv, axis, k):
    n = lax.axis_size(axis)
    return pltpu.make_async_remote_copy(
        src_ref=src, dst_ref=dst, send_sem=send, recv_sem=recv,
        device_id={axis: lax.rem(lax.axis_index(axis) + k, n)},
        device_id_type=pl.DeviceIdType.MESH,
    )


def gather_small_kernel(x_ref, out_ref, send_c, recv_c, send_r, recv_r):
    cols, rows = lax.axis_size("col"), lax.axis_size("row")
    my_col, my_row = lax.axis_index("col"), lax.axis_index("row")
    enter(("col", "row"))
    out_ref[my_row, my_col] = x_ref[...]
    first = [
        push(x_ref, out_ref.at[my_row, my_col], send_c.at[k - 1], recv_c.at[k - 1], "col", k)
        for k in range(1, cols)
    ]
    for copy in first:
        copy.start()
    for copy in first:
        copy.wait()
    second = [
        push(out_ref.at[my_row], out_ref.at[my_row], send_r.at[k - 1], recv_r.at[k - 1], "row", k)
        for k in range(1, rows)
    ]
    for copy in second:
        copy.start()
    for copy in second:
        copy.wait()


def gather_small(x, call_id):
    cols, rows = lax.axis_size("col"), lax.axis_size("row")
    return pl.pallas_call(
        gather_small_kernel,
        out_shape=jax.ShapeDtypeStruct((rows, cols) + x.shape, x.dtype),
        in_specs=[WHOLE],
        out_specs=WHOLE,
        scratch_shapes=[
            pltpu.SemaphoreType.DMA((cols - 1,)), pltpu.SemaphoreType.DMA((cols - 1,)),
            pltpu.SemaphoreType.DMA((rows - 1,)), pltpu.SemaphoreType.DMA((rows - 1,)),
        ],
        compiler_params=pltpu.CompilerParams(collective_id=call_id, has_side_effects=True),
    )(x)


def select_kernel(run, index_ref, x_ref, out_ref):
    def one(b, carry):
        column = pl.multiple_of(index_ref[b] * BLOCK, BLOCK)
        out_ref[b] = x_ref[:, pl.ds(column, BLOCK)]
        return carry

    lax.fori_loop(0, out_ref.shape[0], one, 0, unroll=2)


def select_blocks(index, x):
    count = index.shape[0]
    return pl.pallas_call(
        functools.partial(select_kernel, count),
        out_shape=jax.ShapeDtypeStruct((count, x.shape[0], BLOCK), x.dtype),
        in_specs=[SCALARS, WHOLE],
        out_specs=WHOLE,
    )(index, x)


def exchange_kernel(run, x_ref, out_ref, send, recv):
    n, me = lax.axis_size("col"), lax.axis_index("col")
    enter(("col",))
    copies = []
    for k in range(1, n):
        peer = lax.rem(me + k, n)
        copies.append(
            push(x_ref.at[pl.ds(peer * run, run)], out_ref.at[pl.ds(me * run, run)],
                 send.at[k - 1], recv.at[k - 1], "col", k)
        )
    for copy in copies:
        copy.start()

    def own(i, carry):
        out_ref[me * run + i] = x_ref[me * run + i]
        return carry

    lax.fori_loop(0, run, own, 0)
    for copy in copies:
        copy.wait()


def exchange_blocks(x, call_id):
    n = lax.axis_size("col")
    return pl.pallas_call(
        functools.partial(exchange_kernel, x.shape[0] // n),
        out_shape=jax.ShapeDtypeStruct(x.shape, x.dtype),
        in_specs=[WHOLE],
        out_specs=WHOLE,
        scratch_shapes=[pltpu.SemaphoreType.DMA((n - 1,)), pltpu.SemaphoreType.DMA((n - 1,))],
        compiler_params=pltpu.CompilerParams(collective_id=call_id, has_side_effects=True),
    )(x)


def block_dot(x, e):
    return lax.dot_general(x, e, (((0,), (0,)), ((), ())), preferred_element_type=F32)


def unroll_of(count):
    return math.gcd(count, 4)


def first_terms_kernel(cols_ref, x_ref, t_ref, w_ref, out_ref):
    count = x_ref.shape[0]
    step = unroll_of(count)

    def some(i, carry):
        for j in range(step):
            b = i * step + j
            place = pl.ds(pl.multiple_of(cols_ref[b] * BLOCK, BLOCK), BLOCK)
            e = (t_ref[:, place].astype(F32) * w_ref[...]).astype(BF16)
            out_ref[b] = block_dot(x_ref[b], e).astype(BF16)
        return carry

    lax.fori_loop(0, count // step, some, 0)


def first_terms(cols, x, targets, weight):
    return pl.pallas_call(
        first_terms_kernel,
        out_shape=jax.ShapeDtypeStruct((x.shape[0], BLOCK, BLOCK), BF16),
        in_specs=[SCALARS, WHOLE, WHOLE, WHOLE],
        out_specs=WHOLE,
    )(cols, x, targets, weight)


def next_terms_kernel(cols_ref, scale_ref, x_ref, t_ref, image_ref, w_ref, out_ref):
    count = x_ref.shape[0]
    step = unroll_of(count)
    alpha = scale_ref[0]

    def some(i, carry):
        for j in range(step):
            b = i * step + j
            place = pl.ds(pl.multiple_of(cols_ref[b] * BLOCK, BLOCK), BLOCK)
            left = t_ref[:, place].astype(F32) - alpha * image_ref[:, place]
            out_ref[b] = block_dot(x_ref[b], (left * w_ref[...]).astype(BF16)).astype(BF16)
        return carry

    lax.fori_loop(0, count // step, some, 0)


def next_terms(cols, scale, x, targets, image, weight):
    return pl.pallas_call(
        next_terms_kernel,
        out_shape=jax.ShapeDtypeStruct((x.shape[0], BLOCK, BLOCK), BF16),
        in_specs=[SCALARS, SCALARS, WHOLE, WHOLE, WHOLE, WHOLE],
        out_specs=WHOLE,
    )(cols, scale, x, targets, image, weight)


def sweep_kernel(first, *refs):
    if first:
        (terms_ref, out_ref, own_ref, sums_ref, from_left, from_right, to_right, to_left,
         send_r, recv_r, send_l, recv_l) = refs
        before_ref = None
    else:
        (scale_ref, terms_ref, before_ref, out_ref, own_ref, sums_ref, from_left, from_right,
         to_right, to_left, send_r, recv_r, send_l, recv_l) = refs
        shift = scale_ref[1]
    n, me = lax.axis_size("row"), lax.axis_index("row")
    pieces = send_r.shape[0]
    size = terms_ref.shape[0] // pieces
    share = own_ref.shape[0]
    has_left, has_right = me > 0, me < n - 1
    barrier = pltpu.get_barrier_semaphore()

    def greet(k):
        pl.semaphore_signal(
            barrier, inc=1, device_id={"row": lax.rem(me + k, n)},
            device_id_type=pl.DeviceIdType.MESH,
        )

    pl.when(has_left)(lambda: greet(n - 1))
    pl.when(has_right)(lambda: greet(1))
    pl.semaphore_wait(barrier, has_left.astype(jnp.int32) + has_right.astype(jnp.int32))

    def rightward(src, p):
        place = pl.ds(p * size, size)
        return push(src.at[place], from_left.at[place], send_r.at[p], recv_r.at[p], "row", 1)

    def leftward(src, p):
        place = pl.ds(p * size, size)
        return push(src.at[place], from_right.at[place], send_l.at[p], recv_l.at[p], "row", n - 1)

    def begin(source, heading):
        def one(p, carry):
            heading(source, p).start()
            return carry

        lax.fori_loop(0, pieces, one, 0)

    def clear(buffer):
        def one(i, carry):
            buffer[i] = jnp.zeros((BLOCK, BLOCK), BF16)
            return carry

        lax.fori_loop(0, buffer.shape[0], one, 0)

    @pl.when(me == 0)
    def _():
        begin(terms_ref, rightward)
        clear(from_left)

    @pl.when(me == n - 1)
    def _():
        begin(terms_ref, leftward)
        clear(from_right)

    def add(arrived, staged, p):
        def one(i, carry):
            b = p * size + i
            staged[b] = (arrived[b].astype(F32) + terms_ref[b].astype(F32)).astype(BF16)
            return carry

        lax.fori_loop(0, size, one, 0)

    def total_of(b):
        total = terms_ref[b].astype(F32) + from_left[b].astype(F32) + from_right[b].astype(F32)
        if before_ref is not None:
            total = total - shift * before_ref[b].astype(F32)
        return total

    def pass_right(p):
        @pl.when(has_left)
        def _():
            rightward(to_right, p).wait_recv()

            @pl.when(has_right)
            def _():
                add(from_left, to_right, p)
                rightward(to_right, p).start()

    def pass_left(p):
        @pl.when(has_right)
        def _():
            leftward(to_left, p).wait_recv()

            @pl.when(has_left)
            def _():
                add(from_right, to_left, p)
                leftward(to_left, p).start()

    low = me * 2 < n

    def piece(q, carry):
        @pl.when(q < pieces)
        def _():
            pl.when(low)(lambda: pass_right(q))
            pl.when(jnp.logical_not(low))(lambda: pass_left(q))

        @pl.when(q >= LAG)
        def _():
            p = q - LAG
            pl.when(low)(lambda: pass_left(p))
            pl.when(jnp.logical_not(low))(lambda: pass_right(p))

            def one(i, inner):
                b = p * size + i
                out_ref[b] = total_of(b).astype(BF16)
                return inner

            lax.fori_loop(0, size, one, 0)

        return carry

    lax.fori_loop(0, pieces + LAG, piece, 0)
    sums_ref[...] = jnp.zeros_like(sums_ref)

    def own(i, carry):
        b = me * share + i
        total = total_of(b)
        rounded = total.astype(BF16)
        own_ref[i] = rounded
        wide = rounded.astype(F32)
        sums_ref[0:1, :] += jnp.sum(total * total, axis=0, keepdims=True)
        sums_ref[1:2, :] += jnp.sum(wide * wide, axis=0, keepdims=True)
        if before_ref is not None:
            flat = before_ref[b].astype(F32)
            sums_ref[2:3, :] += jnp.sum(wide * flat, axis=0, keepdims=True)
        return carry

    lax.fori_loop(0, share, own, 0)

    def finish(p, carry):
        pl.when(has_right)(lambda: rightward(to_right, p).wait_send())
        pl.when(has_left)(lambda: leftward(to_left, p).wait_send())
        return carry

    lax.fori_loop(0, pieces, finish, 0)


def sweep(terms, scale, before, call_id):
    n = lax.axis_size("row")
    share = terms.shape[0] // n
    pieces = math.gcd(terms.shape[0], 24)
    first = before is None
    sems = pltpu.SemaphoreType.DMA((pieces,))
    whole = VMEM(terms.shape, BF16)
    return pl.pallas_call(
        functools.partial(sweep_kernel, first),
        out_shape=(
            jax.ShapeDtypeStruct(terms.shape, BF16),
            jax.ShapeDtypeStruct((share, BLOCK, BLOCK), BF16),
            jax.ShapeDtypeStruct((8, LANES), F32),
        ),
        in_specs=[WHOLE] if first else [SCALARS, WHOLE, WHOLE],
        out_specs=(WHOLE, WHOLE, WHOLE),
        scratch_shapes=[whole, whole, whole, whole, sems, sems, sems, sems],
        compiler_params=pltpu.CompilerParams(collective_id=call_id, has_side_effects=True),
    )(*((terms,) if first else (scale, terms, before)))


def apply_kernel(first, cols_ref, x_ref, d_ref, w_ref, *refs):
    if first:
        image_ref, sums_ref = refs
        before_ref = None
    else:
        before_ref, image_ref, sums_ref = refs
    count = x_ref.shape[0]
    step = unroll_of(count)
    columns = image_ref.shape[1] // BLOCK
    samples = image_ref.shape[0]

    def clear(i, carry):
        place = pl.ds(pl.multiple_of(i * BLOCK, BLOCK), BLOCK)
        image_ref[:, place] = jnp.zeros((samples, BLOCK), F32)
        return carry

    lax.fori_loop(0, columns, clear, 0, unroll=2)

    def some(i, carry):
        made = [
            jnp.dot(x_ref[i * step + j], d_ref[i * step + j], preferred_element_type=F32)
            for j in range(step)
        ]
        for j in range(step):
            place = pl.ds(pl.multiple_of(cols_ref[i * step + j] * BLOCK, BLOCK), BLOCK)
            image_ref[:, place] += made[j]
        return carry

    lax.fori_loop(0, count // step, some, 0)
    sums_ref[...] = jnp.zeros_like(sums_ref)

    def measure(i, carry):
        place = pl.ds(pl.multiple_of(i * BLOCK, BLOCK), BLOCK)
        image = image_ref[:, place]
        weighted = w_ref[...] * image
        sums_ref[0:1, :] += jnp.sum(weighted * image, axis=0, keepdims=True)
        if before_ref is not None:
            sums_ref[1:2, :] += jnp.sum(weighted * before_ref[:, place], axis=0, keepdims=True)
        return carry

    lax.fori_loop(0, columns, measure, 0, unroll=2)


def apply_blocks(cols, x, direction, weight, before, taxa):
    first = before is None
    samples = x.shape[1]
    return pl.pallas_call(
        functools.partial(apply_kernel, first),
        out_shape=(
            jax.ShapeDtypeStruct((samples, taxa), F32),
            jax.ShapeDtypeStruct((8, LANES), F32),
        ),
        in_specs=[SCALARS] + [WHOLE] * (3 if first else 4),
        out_specs=(WHOLE, WHOLE),
    )(cols, x, direction, weight, *(() if first else (before,)))


def on_device(samples_x, targets, times, block_rows, block_cols):
    col_count = lax.axis_size("col")
    row_count = lax.axis_size("row")
    taxa_col = samples_x.shape[1]
    sample_count = samples_x.shape[0]
    column_count = taxa_col // BLOCK
    my_col = lax.axis_index("col")
    shard = block_rows.shape[0]
    group_count = shard * row_count
    run = group_count // col_count
    ridge = RIDGE_SHARE * sample_count * row_count
    weight = jnp.broadcast_to(
        (0.5 + times.astype(F32) / T_STEPS)[:, None], (sample_count, BLOCK)
    )
    places = jnp.pad(
        jnp.stack([block_rows, block_cols]), ((0, 6), (0, LANES - shard))
    )
    everywhere = gather_small(places, 1)
    rows_all = everywhere[:, :, 0, :shard].transpose(1, 0, 2).reshape(col_count, group_count)
    wanted = lax.dynamic_slice_in_dim(rows_all, my_col * run, run, 1) - my_col * column_count
    cols_mine = lax.dynamic_index_in_dim(everywhere[:, :, 1, :shard], my_col, 1, keepdims=False)
    cols = cols_mine.reshape(group_count) - my_col * column_count

    x = exchange_blocks(select_blocks(wanted.reshape(-1), samples_x), 2)
    terms = first_terms(cols, x, targets, weight)
    direction, own0, sums0 = sweep(terms, None, None, 3)
    image0, norms0 = apply_blocks(cols, x, direction, weight, None, taxa_col)
    totals = jnp.sum(
        gather_small(jnp.concatenate([sums0[:2], norms0[:1], jnp.zeros((5, LANES), F32)]), 4),
        axis=(0, 1, 3),
    )
    gamma, flat_norm, image_norm = totals[0], totals[1], totals[2]
    alpha0 = gamma / (image_norm + ridge * flat_norm)
    scale = jnp.stack([alpha0, ridge * alpha0])
    terms = next_terms(cols, scale, x, targets, image0, weight)
    spread, own1, sums1 = sweep(terms, scale, direction, 5)
    image1, norms1 = apply_blocks(cols, x, spread, weight, image0, taxa_col)
    totals = jnp.sum(
        gather_small(jnp.concatenate([sums1[:3], norms1[:2], jnp.zeros((3, LANES), F32)]), 6),
        axis=(0, 1, 3),
    )
    beta = totals[0] / gamma
    flat_next = totals[1] + 2.0 * beta * totals[2] + beta * beta * flat_norm
    image_next = totals[3] + 2.0 * beta * totals[4] + beta * beta * image_norm
    alpha1 = totals[0] / (image_next + ridge * flat_next)
    mixed = alpha0 + alpha1 * beta
    coeffs = mixed * own0.astype(F32) + alpha1 * own1.astype(F32)
    residual = targets.astype(F32) - mixed * image0 - alpha1 * image1
    return (coeffs, residual)


def solution(mesh):
    placed = (P("row", "col"), P("row", "col"), P("row"), P(("col", "row")), P(("col", "row")))
    return jax.shard_map(
        on_device,
        mesh=mesh,
        in_specs=placed,
        out_specs=(P(("col", "row"), None, None), P("row", "col")),
        check_vma=False,
    )
```

```python
import functools
import math

import jax
import jax.numpy as jnp
from jax import lax
from jax.experimental import pallas as pl
from jax.experimental.pallas import tpu as pltpu
from jax.sharding import PartitionSpec as P

BLOCK = 128
T_STEPS = 64
RIDGE_SHARE = 0.2
LANES = 128
LAG = 2
VMEM = pltpu.VMEM
F32 = jnp.float32
BF16 = jnp.bfloat16
WHOLE = pl.BlockSpec(memory_space=pltpu.VMEM)
SCALARS = pl.BlockSpec(memory_space=pltpu.SMEM)


def enter(axes):
    barrier = pltpu.get_barrier_semaphore()
    count = 0
    for axis in axes:
        n = lax.axis_size(axis)
        me = lax.axis_index(axis)
        for k in range(1, n):
            pl.semaphore_signal(
                barrier, inc=1, device_id={axis: lax.rem(me + k, n)},
                device_id_type=pl.DeviceIdType.MESH,
            )
        count += n - 1
    pl.semaphore_wait(barrier, count)


def push(src, dst, send, recv, axis, k):
    n = lax.axis_size(axis)
    return pltpu.make_async_remote_copy(
        src_ref=src, dst_ref=dst, send_sem=send, recv_sem=recv,
        device_id={axis: lax.rem(lax.axis_index(axis) + k, n)},
        device_id_type=pl.DeviceIdType.MESH,
    )


def gather_small_kernel(x_ref, out_ref, send_c, recv_c, send_r, recv_r):
    cols, rows = lax.axis_size("col"), lax.axis_size("row")
    my_col, my_row = lax.axis_index("col"), lax.axis_index("row")
    enter(("col", "row"))
    out_ref[my_row, my_col] = x_ref[...]
    first = [
        push(x_ref, out_ref.at[my_row, my_col], send_c.at[k - 1], recv_c.at[k - 1], "col", k)
        for k in range(1, cols)
    ]
    for copy in first:
        copy.start()
    for copy in first:
        copy.wait()
    second = [
        push(out_ref.at[my_row], out_ref.at[my_row], send_r.at[k - 1], recv_r.at[k - 1], "row", k)
        for k in range(1, rows)
    ]
    for copy in second:
        copy.start()
    for copy in second:
        copy.wait()


def gather_small(x, call_id):
    cols, rows = lax.axis_size("col"), lax.axis_size("row")
    return pl.pallas_call(
        gather_small_kernel,
        out_shape=jax.ShapeDtypeStruct((rows, cols) + x.shape, x.dtype),
        in_specs=[WHOLE],
        out_specs=WHOLE,
        scratch_shapes=[
            pltpu.SemaphoreType.DMA((cols - 1,)), pltpu.SemaphoreType.DMA((cols - 1,)),
            pltpu.SemaphoreType.DMA((rows - 1,)), pltpu.SemaphoreType.DMA((rows - 1,)),
        ],
        compiler_params=pltpu.CompilerParams(collective_id=call_id, has_side_effects=True),
    )(x)


def select_kernel(run, index_ref, x_ref, out_ref):
    def one(b, carry):
        column = pl.multiple_of(index_ref[b] * BLOCK, BLOCK)
        out_ref[b] = x_ref[:, pl.ds(column, BLOCK)]
        return carry

    lax.fori_loop(0, out_ref.shape[0], one, 0, unroll=2)


def select_blocks(index, x):
    count = index.shape[0]
    return pl.pallas_call(
        functools.partial(select_kernel, count),
        out_shape=jax.ShapeDtypeStruct((count, x.shape[0], BLOCK), x.dtype),
        in_specs=[SCALARS, WHOLE],
        out_specs=WHOLE,
    )(index, x)


def exchange_kernel(run, x_ref, out_ref, send, recv):
    n, me = lax.axis_size("col"), lax.axis_index("col")
    enter(("col",))
    copies = []
    for k in range(1, n):
        peer = lax.rem(me + k, n)
        copies.append(
            push(x_ref.at[pl.ds(peer * run, run)], out_ref.at[pl.ds(me * run, run)],
                 send.at[k - 1], recv.at[k - 1], "col", k)
        )
    for copy in copies:
        copy.start()

    def own(i, carry):
        out_ref[me * run + i] = x_ref[me * run + i]
        return carry

    lax.fori_loop(0, run, own, 0)
    for copy in copies:
        copy.wait()


def exchange_blocks(x, call_id):
    n = lax.axis_size("col")
    return pl.pallas_call(
        functools.partial(exchange_kernel, x.shape[0] // n),
        out_shape=jax.ShapeDtypeStruct(x.shape, x.dtype),
        in_specs=[WHOLE],
        out_specs=WHOLE,
        scratch_shapes=[pltpu.SemaphoreType.DMA((n - 1,)), pltpu.SemaphoreType.DMA((n - 1,))],
        compiler_params=pltpu.CompilerParams(collective_id=call_id, has_side_effects=True),
    )(x)


def block_dot(x, e):
    return lax.dot_general(x, e, (((0,), (0,)), ((), ())), preferred_element_type=F32)


def unroll_of(count):
    return math.gcd(count, 8)


def first_terms_kernel(cols_ref, x_ref, t_ref, w_ref, out_ref):
    count = x_ref.shape[0]
    step = unroll_of(count)

    def some(i, carry):
        for j in range(step):
            b = i * step + j
            place = pl.ds(pl.multiple_of(cols_ref[b] * BLOCK, BLOCK), BLOCK)
            e = (t_ref[:, place].astype(F32) * w_ref[...]).astype(BF16)
            out_ref[b] = block_dot(x_ref[b], e).astype(BF16)
        return carry

    lax.fori_loop(0, count // step, some, 0)


def first_terms(cols, x, targets, weight):
    return pl.pallas_call(
        first_terms_kernel,
        out_shape=jax.ShapeDtypeStruct((x.shape[0], BLOCK, BLOCK), BF16),
        in_specs=[SCALARS, WHOLE, WHOLE, WHOLE],
        out_specs=WHOLE,
    )(cols, x, targets, weight)


def next_terms_kernel(cols_ref, scale_ref, x_ref, t_ref, image_ref, w_ref, out_ref):
    count = x_ref.shape[0]
    step = unroll_of(count)
    alpha = scale_ref[0]

    def some(i, carry):
        for j in range(step):
            b = i * step + j
            place = pl.ds(pl.multiple_of(cols_ref[b] * BLOCK, BLOCK), BLOCK)
            left = t_ref[:, place].astype(F32) - alpha * image_ref[:, place]
            out_ref[b] = block_dot(x_ref[b], (left * w_ref[...]).astype(BF16)).astype(BF16)
        return carry

    lax.fori_loop(0, count // step, some, 0)


def next_terms(cols, scale, x, targets, image, weight):
    return pl.pallas_call(
        next_terms_kernel,
        out_shape=jax.ShapeDtypeStruct((x.shape[0], BLOCK, BLOCK), BF16),
        in_specs=[SCALARS, SCALARS, WHOLE, WHOLE, WHOLE, WHOLE],
        out_specs=WHOLE,
    )(cols, scale, x, targets, image, weight)


def sweep_kernel(first, *refs):
    if first:
        (terms_ref, out_ref, own_ref, sums_ref, from_left, from_right, to_right, to_left,
         send_r, recv_r, send_l, recv_l) = refs
        before_ref = None
    else:
        (scale_ref, terms_ref, before_ref, out_ref, own_ref, sums_ref, from_left, from_right,
         to_right, to_left, send_r, recv_r, send_l, recv_l) = refs
        shift = scale_ref[1]
    n, me = lax.axis_size("row"), lax.axis_index("row")
    pieces = send_r.shape[0]
    size = terms_ref.shape[0] // pieces
    share = own_ref.shape[0]
    has_left, has_right = me > 0, me < n - 1
    barrier = pltpu.get_barrier_semaphore()

    def greet(k):
        pl.semaphore_signal(
            barrier, inc=1, device_id={"row": lax.rem(me + k, n)},
            device_id_type=pl.DeviceIdType.MESH,
        )

    pl.when(has_left)(lambda: greet(n - 1))
    pl.when(has_right)(lambda: greet(1))
    pl.semaphore_wait(barrier, has_left.astype(jnp.int32) + has_right.astype(jnp.int32))

    def rightward(src, p):
        place = pl.ds(p * size, size)
        return push(src.at[place], from_left.at[place], send_r.at[p], recv_r.at[p], "row", 1)

    def leftward(src, p):
        place = pl.ds(p * size, size)
        return push(src.at[place], from_right.at[place], send_l.at[p], recv_l.at[p], "row", n - 1)

    def begin(source, heading):
        def one(p, carry):
            heading(source, p).start()
            return carry

        lax.fori_loop(0, pieces, one, 0)

    def clear(buffer):
        def one(i, carry):
            buffer[i] = jnp.zeros((BLOCK, BLOCK), BF16)
            return carry

        lax.fori_loop(0, buffer.shape[0], one, 0)

    @pl.when(me == 0)
    def _():
        begin(terms_ref, rightward)
        clear(from_left)

    @pl.when(me == n - 1)
    def _():
        begin(terms_ref, leftward)
        clear(from_right)

    def add(arrived, staged, p):
        def one(i, carry):
            b = p * size + i
            staged[b] = (arrived[b].astype(F32) + terms_ref[b].astype(F32)).astype(BF16)
            return carry

        lax.fori_loop(0, size, one, 0)

    def total_of(b):
        total = terms_ref[b].astype(F32) + from_left[b].astype(F32) + from_right[b].astype(F32)
        if before_ref is not None:
            total = total - shift * before_ref[b].astype(F32)
        return total

    def pass_right(p):
        @pl.when(has_left)
        def _():
            rightward(to_right, p).wait_recv()

            @pl.when(has_right)
            def _():
                add(from_left, to_right, p)
                rightward(to_right, p).start()

    def pass_left(p):
        @pl.when(has_right)
        def _():
            leftward(to_left, p).wait_recv()

            @pl.when(has_left)
            def _():
                add(from_right, to_left, p)
                leftward(to_left, p).start()

    low = me * 2 < n

    def piece(q, carry):
        @pl.when(q < pieces)
        def _():
            pl.when(low)(lambda: pass_right(q))
            pl.when(jnp.logical_not(low))(lambda: pass_left(q))

        @pl.when(q >= LAG)
        def _():
            p = q - LAG
            pl.when(low)(lambda: pass_left(p))
            pl.when(jnp.logical_not(low))(lambda: pass_right(p))

            def one(i, inner):
                b = p * size + i
                out_ref[b] = total_of(b).astype(BF16)
                return inner

            lax.fori_loop(0, size, one, 0)

        return carry

    lax.fori_loop(0, pieces + LAG, piece, 0)
    sums_ref[...] = jnp.zeros_like(sums_ref)

    def own(i, carry):
        b = me * share + i
        total = total_of(b)
        rounded = total.astype(BF16)
        own_ref[i] = rounded
        wide = rounded.astype(F32)
        sums_ref[0:1, :] += jnp.sum(total * total, axis=0, keepdims=True)
        sums_ref[1:2, :] += jnp.sum(wide * wide, axis=0, keepdims=True)
        if before_ref is not None:
            flat = before_ref[b].astype(F32)
            sums_ref[2:3, :] += jnp.sum(wide * flat, axis=0, keepdims=True)
        return carry

    lax.fori_loop(0, share, own, 0)

    def finish(p, carry):
        pl.when(has_right)(lambda: rightward(to_right, p).wait_send())
        pl.when(has_left)(lambda: leftward(to_left, p).wait_send())
        return carry

    lax.fori_loop(0, pieces, finish, 0)


def sweep(terms, scale, before, call_id):
    n = lax.axis_size("row")
    share = terms.shape[0] // n
    pieces = math.gcd(terms.shape[0], 24)
    first = before is None
    sems = pltpu.SemaphoreType.DMA((pieces,))
    whole = VMEM(terms.shape, BF16)
    return pl.pallas_call(
        functools.partial(sweep_kernel, first),
        out_shape=(
            jax.ShapeDtypeStruct(terms.shape, BF16),
            jax.ShapeDtypeStruct((share, BLOCK, BLOCK), BF16),
            jax.ShapeDtypeStruct((8, LANES), F32),
        ),
        in_specs=[WHOLE] if first else [SCALARS, WHOLE, WHOLE],
        out_specs=(WHOLE, WHOLE, WHOLE),
        scratch_shapes=[whole, whole, whole, whole, sems, sems, sems, sems],
        compiler_params=pltpu.CompilerParams(collective_id=call_id, has_side_effects=True),
    )(*((terms,) if first else (scale, terms, before)))


def apply_kernel(first, cols_ref, x_ref, d_ref, w_ref, *refs):
    if first:
        image_ref, sums_ref = refs
        before_ref = None
    else:
        before_ref, image_ref, sums_ref = refs
    count = x_ref.shape[0]
    step = unroll_of(count)
    columns = image_ref.shape[1] // BLOCK
    samples = image_ref.shape[0]

    def clear(i, carry):
        place = pl.ds(pl.multiple_of(i * BLOCK, BLOCK), BLOCK)
        image_ref[:, place] = jnp.zeros((samples, BLOCK), F32)
        return carry

    lax.fori_loop(0, columns, clear, 0, unroll=4)

    def some(i, carry):
        made = [
            jnp.dot(x_ref[i * step + j], d_ref[i * step + j], preferred_element_type=F32)
            for j in range(step)
        ]
        for j in range(step):
            place = pl.ds(pl.multiple_of(cols_ref[i * step + j] * BLOCK, BLOCK), BLOCK)
            image_ref[:, place] += made[j]
        return carry

    lax.fori_loop(0, count // step, some, 0)

    def fold(values):
        return jnp.sum(values.reshape(samples // 8, 8, BLOCK), axis=0)

    def measure(i, carry):
        place = pl.ds(pl.multiple_of(i * BLOCK, BLOCK), BLOCK)
        image = image_ref[:, place]
        weighted = w_ref[...] * image
        square, cross = carry
        square = square + fold(weighted * image)
        if before_ref is not None:
            cross = cross + fold(weighted * before_ref[:, place])
        return square, cross

    empty = jnp.zeros((8, BLOCK), F32)
    square, cross = lax.fori_loop(0, columns, measure, (empty, empty), unroll=4)
    sums_ref[...] = jnp.zeros_like(sums_ref)
    sums_ref[0:1, :] = jnp.sum(square, axis=0, keepdims=True)
    sums_ref[1:2, :] = jnp.sum(cross, axis=0, keepdims=True)


def apply_blocks(cols, x, direction, weight, before, taxa):
    first = before is None
    samples = x.shape[1]
    return pl.pallas_call(
        functools.partial(apply_kernel, first),
        out_shape=(
            jax.ShapeDtypeStruct((samples, taxa), F32),
            jax.ShapeDtypeStruct((8, LANES), F32),
        ),
        in_specs=[SCALARS] + [WHOLE] * (3 if first else 4),
        out_specs=(WHOLE, WHOLE),
    )(cols, x, direction, weight, *(() if first else (before,)))


def on_device(samples_x, targets, times, block_rows, block_cols):
    col_count = lax.axis_size("col")
    row_count = lax.axis_size("row")
    taxa_col = samples_x.shape[1]
    sample_count = samples_x.shape[0]
    column_count = taxa_col // BLOCK
    my_col = lax.axis_index("col")
    shard = block_rows.shape[0]
    group_count = shard * row_count
    run = group_count // col_count
    ridge = RIDGE_SHARE * sample_count * row_count
    weight = jnp.broadcast_to(
        (0.5 + times.astype(F32) / T_STEPS)[:, None], (sample_count, BLOCK)
    )
    places = jnp.pad(
        jnp.stack([block_rows, block_cols]), ((0, 6), (0, LANES - shard))
    )
    everywhere = gather_small(places, 1)
    rows_all = everywhere[:, :, 0, :shard].transpose(1, 0, 2).reshape(col_count, group_count)
    wanted = lax.dynamic_slice_in_dim(rows_all, my_col * run, run, 1) - my_col * column_count
    cols_mine = lax.dynamic_index_in_dim(everywhere[:, :, 1, :shard], my_col, 1, keepdims=False)
    cols = cols_mine.reshape(group_count) - my_col * column_count

    x = exchange_blocks(select_blocks(wanted.reshape(-1), samples_x), 2)
    terms = first_terms(cols, x, targets, weight)
    direction, own0, sums0 = sweep(terms, None, None, 3)
    image0, norms0 = apply_blocks(cols, x, direction, weight, None, taxa_col)
    totals = jnp.sum(
        gather_small(jnp.concatenate([sums0[:2], norms0[:1], jnp.zeros((5, LANES), F32)]), 4),
        axis=(0, 1, 3),
    )
    gamma, flat_norm, image_norm = totals[0], totals[1], totals[2]
    alpha0 = gamma / (image_norm + ridge * flat_norm)
    scale = jnp.stack([alpha0, ridge * alpha0])
    terms = next_terms(cols, scale, x, targets, image0, weight)
    spread, own1, sums1 = sweep(terms, scale, direction, 5)
    image1, norms1 = apply_blocks(cols, x, spread, weight, image0, taxa_col)
    totals = jnp.sum(
        gather_small(jnp.concatenate([sums1[:3], norms1[:2], jnp.zeros((3, LANES), F32)]), 6),
        axis=(0, 1, 3),
    )
    beta = totals[0] / gamma
    flat_next = totals[1] + 2.0 * beta * totals[2] + beta * beta * flat_norm
    image_next = totals[3] + 2.0 * beta * totals[4] + beta * beta * image_norm
    alpha1 = totals[0] / (image_next + ridge * flat_next)
    mixed = alpha0 + alpha1 * beta
    coeffs = mixed * own0.astype(F32) + alpha1 * own1.astype(F32)
    residual = targets.astype(F32) - mixed * image0 - alpha1 * image1
    return (coeffs, residual)


def solution(mesh):
    placed = (P("row", "col"), P("row", "col"), P("row"), P(("col", "row")), P(("col", "row")))
    return jax.shard_map(
        on_device,
        mesh=mesh,
        in_specs=placed,
        out_specs=(P(("col", "row"), None, None), P("row", "col")),
        check_vma=False,
    )
```
